32 devices in a mesh: gx: 2 (over x), gy: 16 (over z, y, core).
Axes of the slice: x: 2, y: 2, z: 4, core: 2. Of those that a mesh axis runs over, the one named last changes fastest.
Arguments:
- offsets: float32 [3, 4, 32, 2, 128], P(None, 'gx', 'gy'), may hold values from 0 to 1
- velocity: float32 [3, 4, 32, 2, 128], P(None, 'gx', 'gy'), may hold values from -6 to 6
- mass: float32 [4, 32, 2, 128], P('gx', 'gy'), may hold values from 0.00390625 to 0.03125
- energy: float32 [4, 32, 2, 128], P('gx', 'gy'), may hold values from 0.3 to 3
- counts: int32 [4, 32, 2], P('gx', 'gy'), may hold values from 1 to 128
Outputs:
- density: float32 [4, 32, 2, 128], P('gx', 'gy')
- acceleration: float32 [3, 4, 32, 2, 128], P(None, 'gx', 'gy')
- heating: float32 [4, 32, 2, 128], P('gx', 'gy')
The draws below stay inside these ranges and needn't reach their ends.
Inputs may be any that keep to these rules, and one draw needn't show every extreme that they name: Slots of a cell from counts on hold no particle.
All inputs are finite; a program needn't handle non-finite values.
Results may differ from the reference program's by a relative error of at most 0.0003.
Values sent between devices are 32-bit elements; how exact they have to be, the bound alone decides.
A program may use at most 64 MiB of HBM per device.

```python
import math
import jax
import jax.numpy as jnp
from jax import lax

P_SIZE = 128
CZ = 2
NX = 4
NY = 32


def set_ends(values, own_key, smallest, top_value):
    spot = [jax.random.randint(jax.random.fold_in(own_key, axis), (), 0, length) for axis, length in enumerate(values.shape)]
    widest = values.shape.index(max(values.shape))
    next_to = spot[:widest] + [(spot[widest] + 1) % values.shape[widest]] + spot[widest + 1:]
    return values.at[tuple(spot)].set(smallest).at[tuple(next_to)].set(top_value)


def steps_of(stream_key, shape, shards, low, top_value):
    factor_of = 1.0
    for dim, shards_of in shards:
        draws = jax.random.uniform(jax.random.fold_in(jax.random.fold_in(stream_key, 6), dim), (shards_of,), jnp.float32, low / len(shards), top_value / len(shards))
        factor_of = factor_of * jnp.repeat(jnp.exp(draws), shape[dim] // shards_of).reshape((-1,) + (1,) * (len(shape) - 1 - dim))
    return factor_of


def normal_values(own_key, extent, deviation, bound, pieces=(), kind=jnp.bfloat16):
    entries = jax.random.normal(own_key, extent, jnp.float32) * deviation
    if len(pieces) > 0:
        entries = steps_of(own_key, extent, pieces, -0.22, 0.18) * entries
    return jnp.clip(entries, min=-bound, max=bound).astype(kind)


def setup_inputs(seed: int = 0) -> dict:
    seeds = jax.random.split(jax.random.key(seed), 6)
    return {
        "offsets": jnp.clip(1.0 * jax.random.uniform(seeds[0], (3, NX, NY, CZ, P_SIZE), jnp.float32) ** steps_of(seeds[0], (3, NX, NY, CZ, P_SIZE), ((1, 2), (2, 16)), -0.2, 0.2), 0.0, 1.0),
        "velocity": normal_values(seeds[1], (3, NX, NY, CZ, P_SIZE), 1.0, 6.0, ((1, 2), (2, 16)), jnp.float32),
        "mass": jnp.clip(jnp.exp(math.log(0.03125) - 2.0794415 * jax.random.uniform(seeds[2], (NX, NY, CZ, P_SIZE), jnp.float32) ** steps_of(seeds[2], (NX, NY, CZ, P_SIZE), ((0, 2), (1, 16)), -0.2, 0.2)), 0.00390625, 0.03125),
        "energy": jnp.clip(jnp.exp(math.log(3.0) - 2.3025851 * jax.random.uniform(seeds[3], (NX, NY, CZ, P_SIZE), jnp.float32) ** steps_of(seeds[3], (NX, NY, CZ, P_SIZE), ((0, 2), (1, 16)), -0.2, 0.2)), 0.3, 3.0),
        "counts": set_ends(jax.random.randint(seeds[4], (NX, NY, CZ), 1, P_SIZE + 1), jax.random.fold_in(seeds[4], 1), 1, P_SIZE).astype(jnp.int32),
    }


SMOOTHING = 0.5
NORMALISE = 1.0 / (math.pi * 0.125)
ADIABATIC = 5.0 / 3.0
VISC_ALPHA = 1.0
VISC_BETA = 2.0
SOFTENING = 0.01

def offsets_list():
    result = []
    for shift_x in (-1, 0, 1):
        for shift_y in (-1, 0, 1):
            for shift_z in (-1, 0, 1):
                result.append((shift_x, shift_y, shift_z))
    return result

def density_terms(own_cell, near_cell, delta):
    step = jnp.asarray(delta, jnp.float32).reshape(3, 1, 1, 1)
    separation = own_cell[0:3, :, :, None] - near_cell[0:3, :, None, :] - step
    scaled = jnp.sqrt(lax.optimization_barrier(jnp.sum(separation * separation, axis=0))) / SMOOTHING
    outer = jnp.maximum(2.0 - scaled, 0.0)
    inner = jnp.maximum(1.0 - scaled, 0.0)
    kernel = NORMALISE * (0.25 * outer * outer * outer - inner * inner * inner)
    return lax.optimization_barrier(jnp.sum(kernel * near_cell[6][:, None, :], axis=-1))

def force_terms(own_cell, near_cell, delta):
    step = jnp.asarray(delta, jnp.float32).reshape(3, 1, 1, 1)
    separation = own_cell[0:3, :, :, None] - near_cell[0:3, :, None, :] - step
    relative = own_cell[3:6, :, :, None] - near_cell[3:6, :, None, :]
    distance_sq = lax.optimization_barrier(jnp.sum(separation * separation, axis=0))
    scaled = jnp.sqrt(distance_sq) / SMOOTHING
    safe_scaled = jnp.where(scaled < 1.0, 1.0, scaled)
    outer = jnp.maximum(2.0 - scaled, 0.0)
    slope = jnp.where(scaled < 1.0, -3.0 + 2.25 * scaled, -0.75 * outer * outer / safe_scaled)
    weight = near_cell[6][:, None, :] * (NORMALISE / (SMOOTHING * SMOOTHING)) * slope
    approach = lax.optimization_barrier(jnp.sum(relative * separation, axis=0))
    closing = SMOOTHING * jnp.minimum(approach, 0.0) / (distance_sq + SOFTENING * SMOOTHING * SMOOTHING)
    sound = 0.5 * (own_cell[8][:, :, None] + near_cell[8][:, None, :])
    mean_rho = 0.5 * (own_cell[9][:, :, None] + near_cell[9][:, None, :])
    viscous = (-VISC_ALPHA * sound * closing + VISC_BETA * closing * closing) / mean_rho
    pushing = weight * (own_cell[7][:, :, None] + near_cell[7][:, None, :] + viscous)
    accel = -lax.optimization_barrier(jnp.sum(pushing[None] * separation, axis=-1))
    heat = lax.optimization_barrier(jnp.sum(weight * (own_cell[7][:, :, None] + 0.5 * viscous) * approach, axis=-1))
    return jnp.concatenate([accel, heat[None]], axis=0)

def block_apply(extended, count_x, count_y, terms, rows_out):
    layers = extended.shape[3] - 2
    slots = extended.shape[4]

    def column(position):
        first = position // count_y
        second = position % count_y
        zero = jnp.zeros((), jnp.int32)
        neighbours = lax.dynamic_slice(extended, (zero, first, second, zero, zero), (extended.shape[0], 3, 3, layers + 2, slots))
        own_cell = neighbours[:, 1, 1, 1:layers + 1]
        total = jnp.zeros((rows_out, layers, slots), jnp.float32)
        for delta in offsets_list():
            near_cell = neighbours[:, 1 + delta[0], 1 + delta[1], 1 + delta[2]:1 + delta[2] + layers]
            total = total + terms(own_cell, near_cell, delta).reshape(rows_out, layers, slots)
        return total
    columns = lax.map(column, jnp.arange(count_x * count_y, dtype=jnp.int32))
    columns = columns.reshape(count_x, count_y, rows_out, layers, slots)
    return jnp.moveaxis(columns, 2, 0)

def force_inputs(particles, density_safe):
    energy_part = particles[7]
    pressure_term = (ADIABATIC - 1.0) * energy_part / density_safe
    sound = jnp.sqrt(ADIABATIC * (ADIABATIC - 1.0) * energy_part)
    return jnp.concatenate([particles[0:7], pressure_term[None], sound[None], density_safe[None]], axis=0)

def reference(offsets, velocity, mass, energy, counts):
    slots = mass.shape[-1]
    occupied = (jnp.arange(slots, dtype=jnp.int32)[None, None, None, :] < counts[..., None]).astype(jnp.float32)
    particles = jnp.concatenate([offsets, velocity, (mass * occupied)[None], energy[None]], axis=0)
    extended = jnp.pad(particles, ((0, 0), (1, 1), (1, 1), (0, 0), (0, 0)), mode='wrap')
    extended = jnp.pad(extended, ((0, 0), (0, 0), (0, 0), (1, 1), (0, 0)))
    count_x = mass.shape[0]
    count_y = mass.shape[1]
    density = block_apply(extended, count_x, count_y, density_terms, 1)[0]
    density_safe = jnp.where(particles[6] > 0.0, density, 1.0)
    density_wide = jnp.pad(density_safe, ((1, 1), (1, 1), (0, 0), (0, 0)), mode='wrap')
    density_wide = jnp.pad(density_wide, ((0, 0), (0, 0), (1, 1), (0, 0)), constant_values=1.0)
    forces = block_apply(force_inputs(extended, density_wide), count_x, count_y, force_terms, 4)
    return (density * occupied, forces[0:3] * occupied[None], forces[3] * occupied)
```

```python
import functools
import math

import jax
import jax.numpy as jnp
from jax import lax
from jax.experimental import pallas as pl
from jax.experimental.pallas import tpu as pltpu
from jax.sharding import PartitionSpec as P

SMOOTHING = 0.5
NORMALISE = 1.0 / (math.pi * 0.125)
ADIABATIC = 5.0 / 3.0
VISC_ALPHA = 1.0
VISC_BETA = 2.0
SOFTENING = 0.01
TINY = 1e-30
VMEM = pltpu.VMEM
MESH = pl.DeviceIdType.MESH
DIRECTIONS = [(dx, dy) for dx in (-1, 0, 1) for dy in (-1, 0, 1) if (dx, dy) != (0, 0)]


def edge(step, count):
    if step == 0:
        return (0, 1, count)
    if step == 1:
        return (count - 1, 0, 1)
    return (0, count + 1, 1)


def exchange_kernel(size_x, size_y, own_ref, out_ref, send_sem, recv_sem, local_sem):
    count_x, count_y = own_ref.shape[0], own_ref.shape[1]
    my_x, my_y = lax.axis_index("gx"), lax.axis_index("gy")
    local = pltpu.make_async_copy(
        own_ref, out_ref.at[pl.ds(1, count_x), pl.ds(1, count_y)], local_sem
    )
    local.start()
    barrier = pltpu.get_barrier_semaphore()
    peers = []
    for dx, dy in DIRECTIONS:
        peers.append((lax.rem(my_x + dx + size_x, size_x), lax.rem(my_y + dy + size_y, size_y)))
    for peer in peers:
        pl.semaphore_signal(barrier, inc=1, device_id=peer, device_id_type=MESH)
    pl.semaphore_wait(barrier, len(peers))
    copies = []
    for k, (dx, dy) in enumerate(DIRECTIONS):
        from_x, to_x, width_x = edge(dx, count_x)
        from_y, to_y, width_y = edge(dy, count_y)
        copy = pltpu.make_async_remote_copy(
            src_ref=own_ref.at[pl.ds(from_x, width_x), pl.ds(from_y, width_y)],
            dst_ref=out_ref.at[pl.ds(to_x, width_x), pl.ds(to_y, width_y)],
            send_sem=send_sem.at[k],
            recv_sem=recv_sem.at[k],
            device_id=peers[k],
            device_id_type=MESH,
        )
        copy.start()
        copies.append(copy)
    local.wait()
    for copy in copies:
        copy.wait()


def exchange(own, collective):
    shape = (own.shape[0] + 2, own.shape[1] + 2) + own.shape[2:]
    sizes = (lax.axis_size("gx"), lax.axis_size("gy"))
    return pl.pallas_call(
        functools.partial(exchange_kernel, *sizes),
        out_shape=jax.ShapeDtypeStruct(shape, own.dtype),
        in_specs=[pl.BlockSpec(memory_space=VMEM)],
        out_specs=pl.BlockSpec(memory_space=VMEM),
        scratch_shapes=[
            pltpu.SemaphoreType.DMA((len(DIRECTIONS),)),
            pltpu.SemaphoreType.DMA((len(DIRECTIONS),)),
            pltpu.SemaphoreType.DMA,
        ],
        compiler_params=pltpu.CompilerParams(collective_id=collective, has_side_effects=True),
        name=f"exchange_{collective}",
    )(own)


def cell_counts(ext_ref, gap):
    size_x, size_y, layers = ext_ref.shape[:3]
    counts, starts, start = {}, {}, jnp.int32(0)
    for x in range(size_x):
        for y in range(size_y):
            for z in range(layers):
                held = jnp.where(ext_ref[x, y, z, 6:7, :] > 0.0, 1.0, 0.0)
                count = jnp.sum(held).astype(jnp.int32)
                counts[x, y, z] = count
                starts[x, y, z] = start
                start = start + (count + 7) // 8 * 8
            starts[x, y, layers] = start
        start = start + gap
    return counts, starts


def base_rows(ext_ref, x, y, z):
    cell = ext_ref[x, y, z]
    rows = lax.broadcasted_iota(jnp.int32, cell.shape, 0)
    shift = jnp.where(rows == 0, float(x), jnp.where(rows == 1, float(y), float(z)))
    placed = (cell + shift) * (1.0 / SMOOTHING)
    return jnp.where(rows < 3, placed, cell)


def fill_lists(features, keys, counts, starts, list_ref, pack_ref, chunk, layers, own):
    for key in keys:
        rows = features(key)
        first = pl.multiple_of(starts[key], 8)
        slots = rows.shape[1]
        list_ref[pl.ds(first, slots), 0 : rows.shape[0]] = rows.T
        if key[1:] == keys[-1][1:]:
            after = pl.multiple_of(first + slots, 8)
            list_ref[pl.ds(after, chunk), :] = jnp.zeros((chunk, list_ref.shape[1]), jnp.float32)
    for column, (x, y) in enumerate(own):
        lower, upper = features((x, y, 0)), features((x, y, 1))
        rolled = pltpu.roll(upper, jnp.bitwise_and(counts[x, y, 0], 127), 1)
        lane = lax.broadcasted_iota(jnp.int32, lower.shape, 1)
        pack_ref[column, 0] = jnp.where(lane < counts[x, y, 0], lower, rolled)
        pack_ref[column, 1] = rolled


def sweep(pair_body, n_sums, column, block_list, starts, x, y, layers, chunk):
    firsts = [starts[x + dx, y - 1, 0] for dx in (-1, 0, 1)]
    ends = [starts[x + dx, y + 1, layers] for dx in (-1, 0, 1)]
    runs = [(end - first + (chunk - 1)) // chunk for first, end in zip(firsts, ends)]

    def body(step, sums):
        row = jnp.where(
            step < runs[0],
            firsts[0] + step * chunk,
            jnp.where(
                step < runs[0] + runs[1],
                firsts[1] + (step - runs[0]) * chunk,
                firsts[2] + (step - runs[0] - runs[1]) * chunk,
            ),
        )
        return pair_body(pl.multiple_of(row, 8), sums)

    width = 128 * block_list
    zeros = tuple(jnp.zeros((8, width), jnp.float32) for _ in range(n_sums))
    sums = lax.fori_loop(0, runs[0] + runs[1] + runs[2], body, zeros)
    return [jnp.sum(s, axis=0, keepdims=True) for s in sums]


def fold(values):
    return jnp.sum(values.reshape(values.shape[0] // 8, 8, values.shape[1]), axis=0)


def unpack(row_a, row_b, count):
    back = jnp.bitwise_and(128 - jnp.bitwise_and(count, 127), 127)
    a = pltpu.roll(jnp.broadcast_to(row_a, (8, 128)), back, 1)[0:1]
    b = pltpu.roll(jnp.broadcast_to(row_b, (8, 128)), back, 1)[0:1]
    lane = lax.broadcasted_iota(jnp.int32, (1, 128), 1)
    upper = jnp.where(lane < 128 - count, a, b)
    return row_a, upper


def run_column(make_body, n_sums, column, total, out_ref, starts, x, y, layers, chunks):
    @pl.when(total > 128)
    def _():
        sums = sweep(make_body(2, chunks[1]), n_sums, column, 2, starts, x, y, layers, chunks[1])
        for k, row in enumerate(sums):
            out_ref[k : k + 1, :] = row

    @pl.when(total <= 128)
    def _():
        sums = sweep(make_body(1, chunks[0]), n_sums, column, 1, starts, x, y, layers, chunks[0])
        for k, row in enumerate(sums):
            out_ref[k : k + 1, 0:128] = row
            out_ref[k : k + 1, 128:256] = jnp.zeros_like(row)


def own_columns(ext_ref):
    return [
        (x, y) for x in range(1, ext_ref.shape[0] - 1) for y in range(1, ext_ref.shape[1] - 1)
    ]


def all_cells(ext_ref):
    size_x, size_y, layers = ext_ref.shape[:3]
    return [(x, y, z) for x in range(size_x) for y in range(size_y) for z in range(layers)]


def wide(pack_ref, column, blocks, row):
    parts = [pack_ref[column, b, row : row + 1, :] for b in range(blocks)]
    return parts[0] if blocks == 1 else jnp.concatenate(parts, axis=1)


def density_kernel(chunks, ext_ref, out_ref, safe_ref, list_ref, pack_ref, sum_ref):
    layers = ext_ref.shape[2]
    counts, starts = cell_counts(ext_ref, max(chunks))
    own = own_columns(ext_ref)
    fill_lists(
        lambda key: base_rows(ext_ref, *key),
        all_cells(ext_ref), counts, starts, list_ref, pack_ref, max(chunks), layers, own,
    )
    for column, (x, y) in enumerate(own):

        def make_body(blocks, chunk, column=column):
            mine = [wide(pack_ref, column, blocks, f) for f in range(3)]

            def body(row, sums):
                near = list_ref[pl.ds(row, chunk), 0:8]
                dist = None
                for f in range(3):
                    gap = mine[f] - near[:, f : f + 1]
                    dist = gap * gap if dist is None else dist + gap * gap
                q = dist * lax.rsqrt(jnp.maximum(dist, TINY))
                outer = jnp.maximum(2.0 - q, 0.0)
                inner = jnp.maximum(1.0 - q, 0.0)
                kernel = outer * outer * outer - 4.0 * (inner * inner * inner)
                return (sums[0] + fold(kernel * near[:, 6:7]),)

            return body

        count = counts[x, y, 0]
        run_column(
            make_body, 1, column, count + counts[x, y, 1], sum_ref, starts, x, y, layers, chunks
        )
        rows = unpack(sum_ref[0:1, 0:128], sum_ref[0:1, 128:256], count)
        for z in range(layers):
            value = rows[z] * (0.25 * NORMALISE)
            held = ext_ref[x, y, z, 6:7, :] > 0.0
            out_ref[x - 1, y - 1, z : z + 1, :] = jnp.where(held, value, 0.0)
            safe_ref[x - 1, y - 1, z : z + 1, :] = jnp.where(held, value, 1.0)


def force_kernel(chunks, ext_ref, rho_ref, accel_ref, heat_ref, feat_ref, list_ref, pack_ref, sum_ref):
    layers = ext_ref.shape[2]
    counts, starts = cell_counts(ext_ref, max(chunks))
    own = own_columns(ext_ref)

    for key in all_cells(ext_ref):
        x, y, z = key
        energy = ext_ref[x, y, z, 7:8, :]
        rho = rho_ref[x, y, z : z + 1, :]
        feat_ref[x, y, z, 0:8, :] = base_rows(ext_ref, x, y, z)
        feat_ref[x, y, z, 7:8, :] = (ADIABATIC - 1.0) * energy / rho
        feat_ref[x, y, z, 8:9, :] = jnp.sqrt(ADIABATIC * (ADIABATIC - 1.0) * energy) * (
            0.5 * VISC_ALPHA / VISC_BETA
        )
        feat_ref[x, y, z, 9:10, :] = rho * (1.0 / VISC_BETA)
        feat_ref[x, y, z, 10:16, :] = jnp.zeros((6, 128), jnp.float32)
    fill_lists(
        lambda key: feat_ref[key],
        all_cells(ext_ref), counts, starts, list_ref, pack_ref, max(chunks), layers, own,
    )
    for column, (x, y) in enumerate(own):

        def make_body(blocks, chunk, column=column):
            mine = [wide(pack_ref, column, blocks, f) for f in range(10)]

            def body(row, sums):
                near = list_ref[pl.ds(row, chunk), 0:16]
                gaps, dist, approach = [], None, None
                for f in range(3):
                    gap = mine[f] - near[:, f : f + 1]
                    speed = mine[3 + f] - near[:, 3 + f : 4 + f]
                    dist = gap * gap if dist is None else dist + gap * gap
                    approach = gap * speed if approach is None else approach + gap * speed
                    gaps.append(gap)
                inverse = lax.rsqrt(jnp.maximum(dist, TINY))
                q = dist * inverse
                outer = jnp.maximum(2.0 - q, 0.0)
                slope = jnp.where(q < 1.0, 4.0 - 3.0 * q, outer * outer * inverse)
                closing = jnp.minimum(approach, 0.0)
                soft = dist + SOFTENING
                sound = mine[8] + near[:, 8:9]
                dense = mine[9] + near[:, 9:10]
                half = closing * (closing - sound * soft) / (soft * soft * dense)
                from_own = mine[7] + half
                both = from_own + (near[:, 7:8] + half)
                weight = near[:, 6:7] * slope
                push = weight * both
                heat = weight * from_own * approach
                return (
                    sums[0] + fold(push * gaps[0]),
                    sums[1] + fold(push * gaps[1]),
                    sums[2] + fold(push * gaps[2]),
                    sums[3] + fold(heat),
                )

            return body

        count = counts[x, y, 0]
        run_column(
            make_body, 4, column, count + counts[x, y, 1], sum_ref, starts, x, y, layers, chunks
        )
        factor = 0.75 * NORMALISE / SMOOTHING
        for k in range(4):
            rows = unpack(sum_ref[k : k + 1, 0:128], sum_ref[k : k + 1, 128:256], count)
            for z in range(layers):
                held = ext_ref[x, y, z, 6:7, :] > 0.0
                if k < 3:
                    accel_ref[k, x - 1, y - 1, z : z + 1, :] = jnp.where(held, rows[z] * factor, 0.0)
                else:
                    heat_ref[x - 1, y - 1, z : z + 1, :] = jnp.where(held, rows[z] * -factor, 0.0)


def shards(offsets, velocity, mass, energy, counts):
    slots = mass.shape[-1]
    count_x, count_y, layers = mass.shape[:3]
    occupied = jnp.arange(slots, dtype=jnp.int32)[None, None, None, :] < counts[..., None]
    held = jnp.where(occupied, mass, 0.0)
    packed = jnp.concatenate([offsets, velocity, held[None], energy[None]], axis=0)
    packed = jnp.moveaxis(packed, 0, 3)
    extended = exchange(packed, 0)
    cells = (count_x + 2) * (count_y + 2) * layers
    own = count_x * count_y
    vmem = pl.BlockSpec(memory_space=VMEM)
    density_chunks, force_chunks = (128, 64), (64, 32)
    density, safe = pl.pallas_call(
        functools.partial(density_kernel, density_chunks),
        out_shape=[jax.ShapeDtypeStruct(mass.shape, jnp.float32)] * 2,
        in_specs=[vmem],
        out_specs=[vmem, vmem],
        scratch_shapes=[
            VMEM((cells * slots + (count_x + 2) * max(density_chunks), 128), jnp.float32),
            VMEM((own, 2, 8, slots), jnp.float32),
            VMEM((8, 2 * slots), jnp.float32),
        ],
        name="density",
    )(extended)
    near = exchange(safe, 1)
    accel, heat = pl.pallas_call(
        functools.partial(force_kernel, force_chunks),
        out_shape=[
            jax.ShapeDtypeStruct((3,) + mass.shape, jnp.float32),
            jax.ShapeDtypeStruct(mass.shape, jnp.float32),
        ],
        in_specs=[vmem, vmem],
        out_specs=[vmem, vmem],
        scratch_shapes=[
            VMEM(extended.shape[:3] + (16, slots), jnp.float32),
            VMEM((cells * slots + (count_x + 2) * max(force_chunks), 128), jnp.float32),
            VMEM((own, 2, 16, slots), jnp.float32),
            VMEM((8, 2 * slots), jnp.float32),
        ],
        name="force",
    )(extended, near)
    return (density, accel, heat)


def solution(mesh):
    in_specs = (
        P(None, "gx", "gy", None, None),
        P(None, "gx", "gy", None, None),
        P("gx", "gy", None, None),
        P("gx", "gy", None, None),
        P("gx", "gy", None),
    )
    out_specs = (
        P("gx", "gy", None, None),
        P(None, "gx", "gy", None, None),
        P("gx", "gy", None, None),
    )
    return jax.shard_map(shards, mesh=mesh, in_specs=in_specs, out_specs=out_specs, check_vma=False)
```

```python
import functools
import math

import jax
import jax.numpy as jnp
from jax import lax
from jax.experimental import pallas as pl
from jax.experimental.pallas import tpu as pltpu
from jax.sharding import PartitionSpec as P

SMOOTHING = 0.5
NORMALISE = 1.0 / (math.pi * 0.125)
ADIABATIC = 5.0 / 3.0
VISC_ALPHA = 1.0
VISC_BETA = 2.0
SOFTENING = 0.01
TINY = 1e-30
VMEM = pltpu.VMEM
MESH = pl.DeviceIdType.MESH
DIRECTIONS = [(dx, dy) for dx in (-1, 0, 1) for dy in (-1, 0, 1) if (dx, dy) != (0, 0)]


def edge(step, count):
    if step == 0:
        return (0, 1, count)
    if step == 1:
        return (count - 1, 0, 1)
    return (0, count + 1, 1)


def start_copies(peers, own_ref, out_ref, count_x, count_y, send_sem, recv_sem):
    copies = []
    for k, (dx, dy) in enumerate(DIRECTIONS):
        from_x, to_x, width_x = edge(dx, count_x)
        from_y, to_y, width_y = edge(dy, count_y)
        copy = pltpu.make_async_remote_copy(
            src_ref=own_ref.at[pl.ds(from_x, width_x), pl.ds(from_y, width_y)],
            dst_ref=out_ref.at[pl.ds(to_x, width_x), pl.ds(to_y, width_y)],
            send_sem=send_sem.at[k],
            recv_sem=recv_sem.at[k],
            device_id=peers[k],
            device_id_type=MESH,
        )
        copy.start()
        copies.append(copy)
    return copies


def segments(x, y, inner_x, inner_y, layers, size_y, own):
    result = []
    for near_x in (x - 1, x, x + 1):
        run = [
            near_y
            for near_y in (y - 1, y, y + 1)
            if (near_x in inner_x and near_y in inner_y) == own
        ]
        for near_y in run:
            first = (near_x * size_y + near_y) * layers
            if result and result[-1][0] + result[-1][1] == first:
                result[-1] = (result[-1][0], result[-1][1] + layers)
            else:
                result.append((first, layers))
    return result


def density_kernel(
    size_gx, size_gy, own_ref, ext_ref, near_ref, list_ref, pack_ref, total_ref, safe_ref,
    send_sem, recv_sem, rho_send, rho_recv, local_sem,
):
    count_x, count_y, layers, _, slots = own_ref.shape
    size_y = count_y + 2
    inner_x, inner_y = range(1, count_x + 1), range(1, count_y + 1)
    own = [(x, y) for x in inner_x for y in inner_y]
    interior = (pl.ds(1, count_x), pl.ds(1, count_y))
    my_x, my_y = lax.axis_index("gx"), lax.axis_index("gy")
    barrier = pltpu.get_barrier_semaphore()
    peers = []
    for dx, dy in DIRECTIONS:
        peers.append(
            (lax.rem(my_x + dx + size_gx, size_gx), lax.rem(my_y + dy + size_gy, size_gy))
        )
    for peer in peers:
        pl.semaphore_signal(barrier, inc=1, device_id=peer, device_id_type=MESH)
    local = pltpu.make_async_copy(own_ref, ext_ref.at[interior], local_sem)
    local.start()
    pl.semaphore_wait(barrier, len(peers))
    copies = start_copies(peers, own_ref, ext_ref, count_x, count_y, send_sem, recv_sem)

    def enter(source, x, y, z, at):
        cell = source[at]
        rows = lax.broadcasted_iota(jnp.int32, cell.shape, 0)
        shift = jnp.where(rows == 0, float(x), jnp.where(rows == 1, float(y), float(z)))
        placed = jnp.where(rows < 3, (cell + shift) * (1.0 / SMOOTHING), cell)
        first = ((x * size_y + y) * layers + z) * slots
        list_ref[first : first + slots, 0:8] = placed.T
        return placed

    def gather(column, runs):
        mine = [
            jnp.concatenate([pack_ref[column, z, f : f + 1, :] for z in range(layers)], axis=1)
            for f in range(3)
        ]

        def body(step, total):
            cell, done = None, 0
            for first, cells in runs:
                here = first + step - done
                cell = here if cell is None else jnp.where(step < done, cell, here)
                done += cells
            near = list_ref[pl.ds(pl.multiple_of(cell * slots, slots), slots), 0:8]
            dist = None
            for f in range(3):
                gap = mine[f] - near[:, f : f + 1]
                dist = gap * gap if dist is None else dist + gap * gap
            q = dist * lax.rsqrt(jnp.maximum(dist, TINY))
            outer = jnp.maximum(2.0 - q, 0.0)
            inner = jnp.maximum(1.0 - q, 0.0)
            kernel = outer * outer * outer - 4.0 * (inner * inner * inner)
            return total + fold(kernel * near[:, 6:7])

        number = sum(cells for _, cells in runs)
        return lax.fori_loop(0, number, body, jnp.zeros((8, layers * slots), jnp.float32))

    for column, (x, y) in enumerate(own):
        for z in range(layers):
            pack_ref[column, z] = enter(own_ref, x, y, z, (x - 1, y - 1, z))
    for column, (x, y) in enumerate(own):
        runs = segments(x, y, inner_x, inner_y, layers, size_y, True)
        total_ref[column] = gather(column, runs)
    for copy in copies:
        copy.wait()
    for x in range(count_x + 2):
        for y in range(count_y + 2):
            if (x, y) not in own:
                for z in range(layers):
                    enter(ext_ref, x, y, z, (x, y, z))
    for column, (x, y) in enumerate(own):
        runs = segments(x, y, inner_x, inner_y, layers, size_y, False)
        total = total_ref[column] + gather(column, runs)
        value = jnp.sum(total, axis=0, keepdims=True) * (0.25 * NORMALISE)
        for z in range(layers):
            held = own_ref[x - 1, y - 1, z, 6:7, :] > 0.0
            row = value[:, z * slots : (z + 1) * slots]
            safe_ref[x - 1, y - 1, z : z + 1, :] = jnp.where(held, row, 1.0)
    local.wait()
    keep = pltpu.make_async_copy(safe_ref, near_ref.at[interior], local_sem)
    keep.start()
    copies = start_copies(peers, safe_ref, near_ref, count_x, count_y, rho_send, rho_recv)
    keep.wait()
    for copy in copies:
        copy.wait()


def cell_counts(ext_ref, gap):
    size_x, size_y, layers = ext_ref.shape[:3]
    counts, starts, start = {}, {}, jnp.int32(0)
    for x in range(size_x):
        for y in range(size_y):
            for z in range(layers):
                held = jnp.where(ext_ref[x, y, z, 6:7, :] > 0.0, 1.0, 0.0)
                count = jnp.sum(held).astype(jnp.int32)
                counts[x, y, z] = count
                starts[x, y, z] = start
                start = start + (count + 7) // 8 * 8
            starts[x, y, layers] = start
        start = start + gap
    return counts, starts


def base_rows(ext_ref, x, y, z):
    cell = ext_ref[x, y, z]
    rows = lax.broadcasted_iota(jnp.int32, cell.shape, 0)
    shift = jnp.where(rows == 0, float(x), jnp.where(rows == 1, float(y), float(z)))
    placed = (cell + shift) * (1.0 / SMOOTHING)
    return jnp.where(rows < 3, placed, cell)


def fill_lists(features, keys, counts, starts, list_ref, pack_ref, chunk, layers, own):
    for key in keys:
        rows = features(key)
        first = pl.multiple_of(starts[key], 8)
        slots = rows.shape[1]
        list_ref[pl.ds(first, slots), 0 : rows.shape[0]] = rows.T
        if key[1:] == keys[-1][1:]:
            after = pl.multiple_of(first + slots, 8)
            list_ref[pl.ds(after, chunk), :] = jnp.zeros((chunk, list_ref.shape[1]), jnp.float32)
    for column, (x, y) in enumerate(own):
        lower, upper = features((x, y, 0)), features((x, y, 1))
        rolled = pltpu.roll(upper, jnp.bitwise_and(counts[x, y, 0], 127), 1)
        lane = lax.broadcasted_iota(jnp.int32, lower.shape, 1)
        pack_ref[column, 0] = jnp.where(lane < counts[x, y, 0], lower, rolled)
        pack_ref[column, 1] = rolled


def sweep(pair_body, n_sums, column, block_list, starts, x, y, layers, chunk):
    firsts = [starts[x + dx, y - 1, 0] for dx in (-1, 0, 1)]
    ends = [starts[x + dx, y + 1, layers] for dx in (-1, 0, 1)]
    runs = [(end - first + (chunk - 1)) // chunk for first, end in zip(firsts, ends)]

    def body(step, sums):
        row = jnp.where(
            step < runs[0],
            firsts[0] + step * chunk,
            jnp.where(
                step < runs[0] + runs[1],
                firsts[1] + (step - runs[0]) * chunk,
                firsts[2] + (step - runs[0] - runs[1]) * chunk,
            ),
        )
        return pair_body(pl.multiple_of(row, 8), sums)

    width = 128 * block_list
    zeros = tuple(jnp.zeros((8, width), jnp.float32) for _ in range(n_sums))
    sums = lax.fori_loop(0, runs[0] + runs[1] + runs[2], body, zeros)
    return [jnp.sum(s, axis=0, keepdims=True) for s in sums]


def fold(values):
    return jnp.sum(values.reshape(values.shape[0] // 8, 8, values.shape[1]), axis=0)


def unpack(row_a, row_b, count):
    back = jnp.bitwise_and(128 - jnp.bitwise_and(count, 127), 127)
    a = pltpu.roll(jnp.broadcast_to(row_a, (8, 128)), back, 1)[0:1]
    b = pltpu.roll(jnp.broadcast_to(row_b, (8, 128)), back, 1)[0:1]
    lane = lax.broadcasted_iota(jnp.int32, (1, 128), 1)
    upper = jnp.where(lane < 128 - count, a, b)
    return row_a, upper


def run_column(make_body, n_sums, column, total, out_ref, starts, x, y, layers, chunks):
    @pl.when(total > 128)
    def _():
        sums = sweep(make_body(2, chunks[1]), n_sums, column, 2, starts, x, y, layers, chunks[1])
        for k, row in enumerate(sums):
            out_ref[k : k + 1, :] = row

    @pl.when(total <= 128)
    def _():
        sums = sweep(make_body(1, chunks[0]), n_sums, column, 1, starts, x, y, layers, chunks[0])
        for k, row in enumerate(sums):
            out_ref[k : k + 1, 0:128] = row
            out_ref[k : k + 1, 128:256] = jnp.zeros_like(row)


def own_columns(ext_ref):
    return [
        (x, y) for x in range(1, ext_ref.shape[0] - 1) for y in range(1, ext_ref.shape[1] - 1)
    ]


def all_cells(ext_ref):
    size_x, size_y, layers = ext_ref.shape[:3]
    return [(x, y, z) for x in range(size_x) for y in range(size_y) for z in range(layers)]


def wide(pack_ref, column, blocks, row):
    parts = [pack_ref[column, b, row : row + 1, :] for b in range(blocks)]
    return parts[0] if blocks == 1 else jnp.concatenate(parts, axis=1)


def force_kernel(
    chunks, ext_ref, rho_ref, density_ref, accel_ref, heat_ref, feat_ref, list_ref, pack_ref, sum_ref
):
    layers = ext_ref.shape[2]
    counts, starts = cell_counts(ext_ref, max(chunks))
    own = own_columns(ext_ref)

    for key in all_cells(ext_ref):
        x, y, z = key
        energy = ext_ref[x, y, z, 7:8, :]
        rho = rho_ref[x, y, z : z + 1, :]
        feat_ref[x, y, z, 0:8, :] = base_rows(ext_ref, x, y, z)
        feat_ref[x, y, z, 7:8, :] = (ADIABATIC - 1.0) * energy / rho
        feat_ref[x, y, z, 8:9, :] = jnp.sqrt(ADIABATIC * (ADIABATIC - 1.0) * energy) * (
            0.5 * VISC_ALPHA / VISC_BETA
        )
        feat_ref[x, y, z, 9:10, :] = rho * (1.0 / VISC_BETA)
        feat_ref[x, y, z, 10:16, :] = jnp.zeros((6, 128), jnp.float32)
    fill_lists(
        lambda key: feat_ref[key],
        all_cells(ext_ref), counts, starts, list_ref, pack_ref, max(chunks), layers, own,
    )
    for column, (x, y) in enumerate(own):

        def make_body(blocks, chunk, column=column):
            mine = [wide(pack_ref, column, blocks, f) for f in range(10)]

            def body(row, sums):
                near = list_ref[pl.ds(row, chunk), 0:16]
                gaps, dist, approach = [], None, None
                for f in range(3):
                    gap = mine[f] - near[:, f : f + 1]
                    speed = mine[3 + f] - near[:, 3 + f : 4 + f]
                    dist = gap * gap if dist is None else dist + gap * gap
                    approach = gap * speed if approach is None else approach + gap * speed
                    gaps.append(gap)
                inverse = lax.rsqrt(jnp.maximum(dist, TINY))
                q = dist * inverse
                outer = jnp.maximum(2.0 - q, 0.0)
                slope = jnp.where(q < 1.0, 4.0 - 3.0 * q, outer * outer * inverse)
                closing = jnp.minimum(approach, 0.0)
                soft = dist + SOFTENING
                sound = mine[8] + near[:, 8:9]
                dense = mine[9] + near[:, 9:10]
                half = closing * (closing - sound * soft) / (soft * soft * dense)
                from_own = mine[7] + half
                both = from_own + (near[:, 7:8] + half)
                weight = near[:, 6:7] * slope
                push = weight * both
                heat = weight * from_own * approach
                return (
                    sums[0] + fold(push * gaps[0]),
                    sums[1] + fold(push * gaps[1]),
                    sums[2] + fold(push * gaps[2]),
                    sums[3] + fold(heat),
                )

            return body

        count = counts[x, y, 0]
        run_column(
            make_body, 4, column, count + counts[x, y, 1], sum_ref, starts, x, y, layers, chunks
        )
        for z in range(layers):
            held = ext_ref[x, y, z, 6:7, :] > 0.0
            density_ref[x - 1, y - 1, z : z + 1, :] = jnp.where(held, rho_ref[x, y, z : z + 1, :], 0.0)
        factor = 0.75 * NORMALISE / SMOOTHING
        for k in range(4):
            rows = unpack(sum_ref[k : k + 1, 0:128], sum_ref[k : k + 1, 128:256], count)
            for z in range(layers):
                held = ext_ref[x, y, z, 6:7, :] > 0.0
                if k < 3:
                    accel_ref[k, x - 1, y - 1, z : z + 1, :] = jnp.where(held, rows[z] * factor, 0.0)
                else:
                    heat_ref[x - 1, y - 1, z : z + 1, :] = jnp.where(held, rows[z] * -factor, 0.0)


def shards(offsets, velocity, mass, energy, counts):
    slots = mass.shape[-1]
    count_x, count_y, layers = mass.shape[:3]
    occupied = jnp.arange(slots, dtype=jnp.int32)[None, None, None, :] < counts[..., None]
    held = jnp.where(occupied, mass, 0.0)
    packed = jnp.concatenate([offsets, velocity, held[None], energy[None]], axis=0)
    packed = jnp.moveaxis(packed, 0, 3)
    wide_x, wide_y = count_x + 2, count_y + 2
    cells = wide_x * wide_y * layers
    own = count_x * count_y
    vmem = pl.BlockSpec(memory_space=VMEM)
    sems = pltpu.SemaphoreType.DMA((len(DIRECTIONS),))
    extended, near = pl.pallas_call(
        functools.partial(density_kernel, lax.axis_size("gx"), lax.axis_size("gy")),
        out_shape=[
            jax.ShapeDtypeStruct((wide_x, wide_y) + packed.shape[2:], jnp.float32),
            jax.ShapeDtypeStruct((wide_x, wide_y, layers, slots), jnp.float32),
        ],
        in_specs=[vmem],
        out_specs=[vmem, vmem],
        scratch_shapes=[
            VMEM((cells * slots, 128), jnp.float32),
            VMEM((own, layers, 8, slots), jnp.float32),
            VMEM((own, 8, layers * slots), jnp.float32),
            VMEM((count_x, count_y, layers, slots), jnp.float32),
            sems,
            sems,
            sems,
            sems,
            pltpu.SemaphoreType.DMA,
        ],
        compiler_params=pltpu.CompilerParams(collective_id=0, has_side_effects=True),
        name="density",
    )(packed)
    force_chunks = (128, 64)
    density, accel, heat = pl.pallas_call(
        functools.partial(force_kernel, force_chunks),
        out_shape=[
            jax.ShapeDtypeStruct(mass.shape, jnp.float32),
            jax.ShapeDtypeStruct((3,) + mass.shape, jnp.float32),
            jax.ShapeDtypeStruct(mass.shape, jnp.float32),
        ],
        in_specs=[vmem, vmem],
        out_specs=[vmem, vmem, vmem],
        scratch_shapes=[
            VMEM((wide_x, wide_y, layers, 16, slots), jnp.float32),
            VMEM((cells * slots + wide_x * max(force_chunks), 128), jnp.float32),
            VMEM((own, 2, 16, slots), jnp.float32),
            VMEM((8, 2 * slots), jnp.float32),
        ],
        name="force",
    )(extended, near)
    return (density, accel, heat)


def solution(mesh):
    in_specs = (
        P(None, "gx", "gy", None, None),
        P(None, "gx", "gy", None, None),
        P("gx", "gy", None, None),
        P("gx", "gy", None, None),
        P("gx", "gy", None),
    )
    out_specs = (
        P("gx", "gy", None, None),
        P(None, "gx", "gy", None, None),
        P("gx", "gy", None, None),
    )
    return jax.shard_map(shards, mesh=mesh, in_specs=in_specs, out_specs=out_specs, check_vma=False)
```

```python
import functools
import math

import jax
import jax.numpy as jnp
from jax import lax
from jax.experimental import pallas as pl
from jax.experimental.pallas import tpu as pltpu
from jax.sharding import PartitionSpec as P

SMOOTHING = 0.5
NORMALISE = 1.0 / (math.pi * 0.125)
ADIABATIC = 5.0 / 3.0
VISC_ALPHA = 1.0
VISC_BETA = 2.0
SOFTENING = 0.01
TINY = 1e-30
VMEM = pltpu.VMEM
MESH = pl.DeviceIdType.MESH
DIRECTIONS = [(dx, dy) for dx in (-1, 0, 1) for dy in (-1, 0, 1) if (dx, dy) != (0, 0)]


def edge(step, count):
    if step == 0:
        return (0, 1, count)
    if step == 1:
        return (count - 1, 0, 1)
    return (0, count + 1, 1)


def start_copies(peers, own_ref, out_ref, count_x, count_y, send_sem, recv_sem):
    copies = []
    for k, (dx, dy) in enumerate(DIRECTIONS):
        from_x, to_x, width_x = edge(dx, count_x)
        from_y, to_y, width_y = edge(dy, count_y)
        copy = pltpu.make_async_remote_copy(
            src_ref=own_ref.at[pl.ds(from_x, width_x), pl.ds(from_y, width_y)],
            dst_ref=out_ref.at[pl.ds(to_x, width_x), pl.ds(to_y, width_y)],
            send_sem=send_sem.at[k],
            recv_sem=recv_sem.at[k],
            device_id=peers[k],
            device_id_type=MESH,
        )
        copy.start()
        copies.append(copy)
    return copies


def segments(x, y, inner_x, inner_y, layers, size_y, own):
    result = []
    for near_x in (x - 1, x, x + 1):
        run = [
            near_y
            for near_y in (y - 1, y, y + 1)
            if (near_x in inner_x and near_y in inner_y) == own
        ]
        for near_y in run:
            first = (near_x * size_y + near_y) * layers
            if result and result[-1][0] + result[-1][1] == first:
                result[-1] = (result[-1][0], result[-1][1] + layers)
            else:
                result.append((first, layers))
    return result


def density_kernel(
    size_gx, size_gy, offsets_hbm, velocity_hbm, mass_hbm, energy_hbm, counts_ref,
    ext_ref, near_ref, part_ref,
    offsets_ref, velocity_ref, mass_ref, energy_ref, own_ref,
    list_ref, pack_ref, total_ref, safe_ref,
    send_sem, recv_sem, rho_send, rho_recv, local_sem, in_sem,
):
    count_x, count_y, layers, _, slots = own_ref.shape
    size_y = count_y + 2
    inner_x, inner_y = range(1, count_x + 1), range(1, count_y + 1)
    own = [(x, y) for x in inner_x for y in inner_y]
    interior = (pl.ds(1, count_x), pl.ds(1, count_y))
    my_x, my_y = lax.axis_index("gx"), lax.axis_index("gy")
    barrier = pltpu.get_barrier_semaphore()
    peers = []
    for dx, dy in DIRECTIONS:
        peers.append(
            (lax.rem(my_x + dx + size_gx, size_gx), lax.rem(my_y + dy + size_gy, size_gy))
        )
    for peer in peers:
        pl.semaphore_signal(barrier, inc=1, device_id=peer, device_id_type=MESH)
    sources = (offsets_hbm, velocity_hbm, mass_hbm, energy_hbm)
    targets = (offsets_ref, velocity_ref, mass_ref, energy_ref)
    loads = [pltpu.make_async_copy(a, b, in_sem.at[k]) for k, (a, b) in enumerate(zip(sources, targets))]
    for load in loads:
        load.start()
    for load in loads:
        load.wait()
    lane = lax.broadcasted_iota(jnp.int32, (1, slots), 1)
    for x in range(count_x):
        for y in range(count_y):
            for z in range(layers):
                at = slice(z, z + 1)
                for f in range(3):
                    own_ref[x, y, z, f : f + 1, :] = offsets_ref[f, x, y, at, :]
                    own_ref[x, y, z, 3 + f : 4 + f, :] = velocity_ref[f, x, y, at, :]
                own_ref[x, y, z, 6:7, :] = jnp.where(
                    lane < counts_ref[x, y, z], mass_ref[x, y, at, :], 0.0
                )
                own_ref[x, y, z, 7:8, :] = energy_ref[x, y, at, :]
    local = pltpu.make_async_copy(own_ref, ext_ref.at[interior], local_sem)
    local.start()
    pl.semaphore_wait(barrier, len(peers))
    copies = start_copies(peers, own_ref, ext_ref, count_x, count_y, send_sem, recv_sem)

    def enter(source, x, y, z, at):
        cell = source[at]
        rows = lax.broadcasted_iota(jnp.int32, cell.shape, 0)
        shift = jnp.where(rows == 0, float(x), jnp.where(rows == 1, float(y), float(z)))
        placed = jnp.where(rows < 3, (cell + shift) * (1.0 / SMOOTHING), cell)
        first = ((x * size_y + y) * layers + z) * slots
        list_ref[first : first + slots, 0:8] = placed.T
        return placed

    def gather(column, runs):
        mine = [
            jnp.concatenate([pack_ref[column, z, f : f + 1, :] for z in range(layers)], axis=1)
            for f in range(3)
        ]

        def body(step, total):
            cell, done = None, 0
            for first, cells in runs:
                here = first + step - done
                cell = here if cell is None else jnp.where(step < done, cell, here)
                done += cells
            near = list_ref[pl.ds(pl.multiple_of(cell * slots, slots), slots), 0:8]
            dist = None
            for f in range(3):
                gap = mine[f] - near[:, f : f + 1]
                dist = gap * gap if dist is None else dist + gap * gap
            q = dist * lax.rsqrt(jnp.maximum(dist, TINY))
            outer = jnp.maximum(2.0 - q, 0.0)
            inner = jnp.maximum(1.0 - q, 0.0)
            kernel = outer * outer * outer - 4.0 * (inner * inner * inner)
            return total + fold(kernel * near[:, 6:7])

        number = sum(cells for _, cells in runs)
        return lax.fori_loop(0, number, body, jnp.zeros((8, layers * slots), jnp.float32))

    for column, (x, y) in enumerate(own):
        for z in range(layers):
            pack_ref[column, z, 0:8, :] = enter(own_ref, x, y, z, (x - 1, y - 1, z))
    for column, (x, y) in enumerate(own):
        runs = segments(x, y, inner_x, inner_y, layers, size_y, True)
        total_ref[column] = gather(column, runs)
    for copy in copies:
        copy.wait()
    for x in range(count_x + 2):
        for y in range(count_y + 2):
            if (x, y) not in own:
                for z in range(layers):
                    enter(ext_ref, x, y, z, (x, y, z))
    for column, (x, y) in enumerate(own):
        runs = segments(x, y, inner_x, inner_y, layers, size_y, False)
        total = total_ref[column] + gather(column, runs)
        value = jnp.sum(total, axis=0, keepdims=True) * (0.25 * NORMALISE)
        for z in range(layers):
            held = own_ref[x - 1, y - 1, z, 6:7, :] > 0.0
            row = value[:, z * slots : (z + 1) * slots]
            safe_ref[x - 1, y - 1, z : z + 1, :] = jnp.where(held, row, 1.0)
    local.wait()
    keep = pltpu.make_async_copy(safe_ref, near_ref.at[interior], local_sem)
    keep.start()
    copies = start_copies(peers, safe_ref, near_ref, count_x, count_y, rho_send, rho_recv)
    for x, y in own:
        for z in range(layers):
            index = (x - 1) * count_y + y - 1
            energy = own_ref[x - 1, y - 1, z, 7:8, :]
            pack_ref[index, z, 7:16, :] = thermal_rows(energy, safe_ref[x - 1, y - 1, z : z + 1, :])
            first = ((x * size_y + y) * layers + z) * slots
            list_ref[first : first + slots, 0:16] = pack_ref[index, z].T
    for column, (x, y) in enumerate(own):
        near_y = [b for b in (y - 1, y, y + 1) if b in inner_y]
        base = (x * size_y + near_y[0]) * layers
        mine = [
            jnp.concatenate([pack_ref[column, z, f : f + 1, :] for z in range(layers)], axis=1)
            for f in range(10)
        ]

        def body(step, sums, base=base, mine=mine):
            row = pl.multiple_of((base + step) * slots, slots)
            near = list_ref[pl.ds(row, slots), 0:16]
            return force_sums(mine, near, near[:, 6:7], sums)

        zeros = tuple(jnp.zeros((8, layers * slots), jnp.float32) for _ in range(4))
        sums = lax.fori_loop(0, len(near_y) * layers, body, zeros)
        for k in range(4):
            part_ref[column, k : k + 1, :] = jnp.sum(sums[k], axis=0, keepdims=True)
        part_ref[column, 4:8, :] = jnp.zeros((4, layers * slots), jnp.float32)
    keep.wait()
    for copy in copies:
        copy.wait()


def thermal_rows(energy, rho):
    return jnp.concatenate(
        [
            (ADIABATIC - 1.0) * energy / rho,
            jnp.sqrt(ADIABATIC * (ADIABATIC - 1.0) * energy) * (0.5 * VISC_ALPHA / VISC_BETA),
            rho * (1.0 / VISC_BETA),
            jnp.zeros((6, energy.shape[1]), jnp.float32),
        ],
        axis=0,
    )


def force_sums(mine, near, mass, sums):
    gaps, dist, approach = [], None, None
    for f in range(3):
        gap = mine[f] - near[:, f : f + 1]
        speed = mine[3 + f] - near[:, 3 + f : 4 + f]
        dist = gap * gap if dist is None else dist + gap * gap
        approach = gap * speed if approach is None else approach + gap * speed
        gaps.append(gap)
    inverse = lax.rsqrt(jnp.maximum(dist, TINY))
    q = dist * inverse
    outer = jnp.maximum(2.0 - q, 0.0)
    slope = jnp.where(q < 1.0, 4.0 - 3.0 * q, outer * outer * inverse)
    closing = jnp.minimum(approach, 0.0)
    soft = dist + SOFTENING
    sound = mine[8] + near[:, 8:9]
    dense = mine[9] + near[:, 9:10]
    half = closing * (closing - sound * soft) / (soft * soft * dense)
    from_own = mine[7] + half
    both = from_own + (near[:, 7:8] + half)
    weight = mass * slope
    push = weight * both
    heat = weight * from_own * approach
    return (
        sums[0] + fold(push * gaps[0]),
        sums[1] + fold(push * gaps[1]),
        sums[2] + fold(push * gaps[2]),
        sums[3] + fold(heat),
    )


def cell_counts(ext_ref, gap):
    size_x, size_y, layers = ext_ref.shape[:3]
    counts, starts, start = {}, {}, jnp.int32(0)
    for x in range(size_x):
        for y in range(size_y):
            for z in range(layers):
                held = jnp.where(ext_ref[x, y, z, 6:7, :] > 0.0, 1.0, 0.0)
                count = jnp.sum(held).astype(jnp.int32)
                counts[x, y, z] = count
                starts[x, y, z] = start
                start = start + (count + 7) // 8 * 8
            starts[x, y, layers] = start
        start = start + gap
    return counts, starts


def base_rows(ext_ref, x, y, z):
    cell = ext_ref[x, y, z]
    rows = lax.broadcasted_iota(jnp.int32, cell.shape, 0)
    shift = jnp.where(rows == 0, float(x), jnp.where(rows == 1, float(y), float(z)))
    placed = (cell + shift) * (1.0 / SMOOTHING)
    return jnp.where(rows < 3, placed, cell)


def fill_lists(features, keys, counts, starts, list_ref, pack_ref, chunk, layers, own):
    for key in keys:
        rows = features(key)
        first = pl.multiple_of(starts[key], 8)
        slots = rows.shape[1]
        list_ref[pl.ds(first, slots), 0 : rows.shape[0]] = rows.T
        if key[1:] == keys[-1][1:]:
            after = pl.multiple_of(first + slots, 8)
            list_ref[pl.ds(after, chunk), :] = jnp.zeros((chunk, list_ref.shape[1]), jnp.float32)
    for column, (x, y) in enumerate(own):
        lower, upper = features((x, y, 0)), features((x, y, 1))
        rolled = pltpu.roll(upper, jnp.bitwise_and(counts[x, y, 0], 127), 1)
        lane = lax.broadcasted_iota(jnp.int32, lower.shape, 1)
        pack_ref[column, 0] = jnp.where(lane < counts[x, y, 0], lower, rolled)
        pack_ref[column, 1] = rolled


def sweep(pair_body, n_sums, block_list, starts, x, y, inner_y, layers, chunk):
    spans = []
    for near_x in (x - 1, x, x + 1):
        skip = inner_y if near_x == x else ()
        for near_y in (y - 1, y, y + 1):
            if near_y in skip:
                continue
            first, end = starts[near_x, near_y, 0], starts[near_x, near_y, layers]
            if spans and spans[-1][0] == (near_x, near_y - 1):
                spans[-1] = ((near_x, near_y), spans[-1][1], end)
            else:
                spans.append(((near_x, near_y), first, end))
    total, below = jnp.int32(0), []
    for _, first, end in spans:
        below.append(total)
        total = total + (end - first + (chunk - 1)) // chunk

    def body(step, sums):
        row, last = spans[0][1] + step * chunk, spans[0][2]
        for before, (_, first, end) in zip(below[1:], spans[1:]):
            row = jnp.where(step < before, row, first + (step - before) * chunk)
            last = jnp.where(step < before, last, end)
        return pair_body(pl.multiple_of(row, 8), last, sums)

    width = 128 * block_list
    zeros = tuple(jnp.zeros((8, width), jnp.float32) for _ in range(n_sums))
    sums = lax.fori_loop(0, total, body, zeros)
    return [jnp.sum(s, axis=0, keepdims=True) for s in sums]


def fold(values):
    return jnp.sum(values.reshape(values.shape[0] // 8, 8, values.shape[1]), axis=0)


def unpack(row_a, row_b, count):
    back = jnp.bitwise_and(128 - jnp.bitwise_and(count, 127), 127)
    a = pltpu.roll(jnp.broadcast_to(row_a, (8, 128)), back, 1)[0:1]
    b = pltpu.roll(jnp.broadcast_to(row_b, (8, 128)), back, 1)[0:1]
    lane = lax.broadcasted_iota(jnp.int32, (1, 128), 1)
    upper = jnp.where(lane < 128 - count, a, b)
    return row_a, upper


def run_column(make_body, n_sums, total, out_ref, starts, x, y, inner_y, layers, chunks):
    @pl.when(total > 128)
    def _():
        sums = sweep(make_body(2, chunks[1]), n_sums, 2, starts, x, y, inner_y, layers, chunks[1])
        for k, row in enumerate(sums):
            out_ref[k : k + 1, :] = row

    @pl.when(total <= 128)
    def _():
        sums = sweep(make_body(1, chunks[0]), n_sums, 1, starts, x, y, inner_y, layers, chunks[0])
        for k, row in enumerate(sums):
            out_ref[k : k + 1, 0:128] = row
            out_ref[k : k + 1, 128:256] = jnp.zeros_like(row)


def own_columns(ext_ref):
    return [
        (x, y) for x in range(1, ext_ref.shape[0] - 1) for y in range(1, ext_ref.shape[1] - 1)
    ]


def all_cells(ext_ref):
    size_x, size_y, layers = ext_ref.shape[:3]
    return [(x, y, z) for x in range(size_x) for y in range(size_y) for z in range(layers)]


def wide(pack_ref, column, blocks, row):
    parts = [pack_ref[column, b, row : row + 1, :] for b in range(blocks)]
    return parts[0] if blocks == 1 else jnp.concatenate(parts, axis=1)


def force_kernel(
    chunks, ext_ref, rho_ref, part_ref, density_ref, accel_ref, heat_ref, feat_ref, list_ref, pack_ref, sum_ref
):
    layers = ext_ref.shape[2]
    counts, starts = cell_counts(ext_ref, max(chunks))
    own = own_columns(ext_ref)
    inner_y = range(1, ext_ref.shape[1] - 1)

    for key in all_cells(ext_ref):
        x, y, z = key
        energy = ext_ref[x, y, z, 7:8, :]
        rho = rho_ref[x, y, z : z + 1, :]
        feat_ref[x, y, z, 0:8, :] = base_rows(ext_ref, x, y, z)
        feat_ref[x, y, z, 7:16, :] = thermal_rows(energy, rho)
    fill_lists(
        lambda key: feat_ref[key],
        all_cells(ext_ref), counts, starts, list_ref, pack_ref, max(chunks), layers, own,
    )
    for column, (x, y) in enumerate(own):

        def make_body(blocks, chunk, column=column):
            mine = [wide(pack_ref, column, blocks, f) for f in range(10)]

            def body(row, end, sums):
                near = list_ref[pl.ds(row, chunk), 0:16]
                place = lax.broadcasted_iota(jnp.int32, near.shape, 0)
                mass = jnp.where(place < end - row, near, 0.0)[:, 6:7]
                return force_sums(mine, near, mass, sums)

            return body

        count = counts[x, y, 0]
        run_column(
            make_body, 4, count + counts[x, y, 1], sum_ref, starts, x, y, inner_y, layers, chunks
        )
        for z in range(layers):
            held = ext_ref[x, y, z, 6:7, :] > 0.0
            density_ref[x - 1, y - 1, z : z + 1, :] = jnp.where(held, rho_ref[x, y, z : z + 1, :], 0.0)
        factor = 0.75 * NORMALISE / SMOOTHING
        for k in range(4):
            rows = unpack(sum_ref[k : k + 1, 0:128], sum_ref[k : k + 1, 128:256], count)
            for z in range(layers):
                held = ext_ref[x, y, z, 6:7, :] > 0.0
                value = rows[z] + part_ref[column, k : k + 1, z * 128 : (z + 1) * 128]
                if k < 3:
                    accel_ref[k, x - 1, y - 1, z : z + 1, :] = jnp.where(held, value * factor, 0.0)
                else:
                    heat_ref[x - 1, y - 1, z : z + 1, :] = jnp.where(held, value * -factor, 0.0)


def shards(offsets, velocity, mass, energy, counts):
    slots = mass.shape[-1]
    count_x, count_y, layers = mass.shape[:3]
    wide_x, wide_y = count_x + 2, count_y + 2
    cells = wide_x * wide_y * layers
    own = count_x * count_y
    vmem = pl.BlockSpec(memory_space=VMEM)
    sems = pltpu.SemaphoreType.DMA((len(DIRECTIONS),))
    own_shape = (count_x, count_y, layers, 8, slots)
    extended, near, part = pl.pallas_call(
        functools.partial(density_kernel, lax.axis_size("gx"), lax.axis_size("gy")),
        out_shape=[
            jax.ShapeDtypeStruct((wide_x, wide_y) + own_shape[2:], jnp.float32),
            jax.ShapeDtypeStruct((wide_x, wide_y, layers, slots), jnp.float32),
            jax.ShapeDtypeStruct((own, 8, layers * slots), jnp.float32),
        ],
        in_specs=[pl.BlockSpec(memory_space=pl.ANY)] * 4 + [pl.BlockSpec(memory_space=pltpu.SMEM)],
        out_specs=[vmem, vmem, vmem],
        scratch_shapes=[
            VMEM(offsets.shape, jnp.float32),
            VMEM(velocity.shape, jnp.float32),
            VMEM(mass.shape, jnp.float32),
            VMEM(energy.shape, jnp.float32),
            VMEM(own_shape, jnp.float32),
            VMEM((cells * slots, 128), jnp.float32),
            VMEM((own, layers, 16, slots), jnp.float32),
            VMEM((own, 8, layers * slots), jnp.float32),
            VMEM((count_x, count_y, layers, slots), jnp.float32),
            sems,
            sems,
            sems,
            sems,
            pltpu.SemaphoreType.DMA,
            pltpu.SemaphoreType.DMA((4,)),
        ],
        compiler_params=pltpu.CompilerParams(collective_id=0, has_side_effects=True),
        name="density",
    )(offsets, velocity, mass, energy, counts)
    force_chunks = (128, 64)
    density, accel, heat = pl.pallas_call(
        functools.partial(force_kernel, force_chunks),
        out_shape=[
            jax.ShapeDtypeStruct(mass.shape, jnp.float32),
            jax.ShapeDtypeStruct((3,) + mass.shape, jnp.float32),
            jax.ShapeDtypeStruct(mass.shape, jnp.float32),
        ],
        in_specs=[vmem, vmem, vmem],
        out_specs=[vmem, vmem, vmem],
        scratch_shapes=[
            VMEM((wide_x, wide_y, layers, 16, slots), jnp.float32),
            VMEM((cells * slots + wide_x * max(force_chunks), 128), jnp.float32),
            VMEM((own, 2, 16, slots), jnp.float32),
            VMEM((8, 2 * slots), jnp.float32),
        ],
        name="force",
    )(extended, near, part)
    return (density, accel, heat)


def solution(mesh):
    in_specs = (
        P(None, "gx", "gy", None, None),
        P(None, "gx", "gy", None, None),
        P("gx", "gy", None, None),
        P("gx", "gy", None, None),
        P("gx", "gy", None),
    )
    out_specs = (
        P("gx", "gy", None, None),
        P(None, "gx", "gy", None, None),
        P("gx", "gy", None, None),
    )
    return jax.shard_map(shards, mesh=mesh, in_specs=in_specs, out_specs=out_specs, check_vma=False)
```

```python
import functools
import math

import jax
import jax.numpy as jnp
from jax import lax
from jax.experimental import pallas as pl
from jax.experimental.pallas import tpu as pltpu
from jax.sharding import PartitionSpec as P

SMOOTHING = 0.5
NORMALISE = 1.0 / (math.pi * 0.125)
ADIABATIC = 5.0 / 3.0
VISC_ALPHA = 1.0
VISC_BETA = 2.0
SOFTENING = 0.01
TINY = 1e-30
VMEM = pltpu.VMEM
MESH = pl.DeviceIdType.MESH
DIRECTIONS = [(dx, dy) for dx in (-1, 0, 1) for dy in (-1, 0, 1) if (dx, dy) != (0, 0)]


def edge(step, count):
    if step == 0:
        return (0, 1, count)
    if step == 1:
        return (count - 1, 0, 1)
    return (0, count + 1, 1)


def start_copies(peers, own_ref, out_ref, count_x, count_y, send_sem, recv_sem):
    copies = []
    for k, (dx, dy) in enumerate(DIRECTIONS):
        from_x, to_x, width_x = edge(dx, count_x)
        from_y, to_y, width_y = edge(dy, count_y)
        copy = pltpu.make_async_remote_copy(
            src_ref=own_ref.at[pl.ds(from_x, width_x), pl.ds(from_y, width_y)],
            dst_ref=out_ref.at[pl.ds(to_x, width_x), pl.ds(to_y, width_y)],
            send_sem=send_sem.at[k],
            recv_sem=recv_sem.at[k],
            device_id=peers[k],
            device_id_type=MESH,
        )
        copy.start()
        copies.append(copy)
    return copies


def segments(x, y, inner_x, inner_y, layers, size_y, own):
    result = []
    for near_x in (x - 1, x, x + 1):
        run = [
            near_y
            for near_y in (y - 1, y, y + 1)
            if (near_x in inner_x and near_y in inner_y) == own
        ]
        for near_y in run:
            first = (near_x * size_y + near_y) * layers
            if result and result[-1][0] + result[-1][1] == first:
                result[-1] = (result[-1][0], result[-1][1] + layers)
            else:
                result.append((first, layers))
    return result


def density_kernel(
    size_gx, size_gy, offsets_hbm, velocity_hbm, mass_hbm, energy_hbm, counts_ref,
    ext_ref, near_ref, part_ref,
    offsets_ref, velocity_ref, mass_ref, energy_ref, own_ref,
    list_ref, pack_ref, total_ref, safe_ref,
    send_sem, recv_sem, rho_send, rho_recv, local_sem, in_sem,
):
    count_x, count_y, layers, _, slots = own_ref.shape
    size_y = count_y + 2
    inner_x, inner_y = range(1, count_x + 1), range(1, count_y + 1)
    own = [(x, y) for x in inner_x for y in inner_y]
    interior = (pl.ds(1, count_x), pl.ds(1, count_y))
    my_x, my_y = lax.axis_index("gx"), lax.axis_index("gy")
    barrier = pltpu.get_barrier_semaphore()
    peers = []
    for dx, dy in DIRECTIONS:
        peers.append(
            (lax.rem(my_x + dx + size_gx, size_gx), lax.rem(my_y + dy + size_gy, size_gy))
        )
    for peer in peers:
        pl.semaphore_signal(barrier, inc=1, device_id=peer, device_id_type=MESH)
    sources = (offsets_hbm, velocity_hbm, mass_hbm, energy_hbm)
    targets = (offsets_ref, velocity_ref, mass_ref, energy_ref)
    loads = [pltpu.make_async_copy(a, b, in_sem.at[k]) for k, (a, b) in enumerate(zip(sources, targets))]
    for load in loads:
        load.start()
    for load in loads:
        load.wait()
    lane = lax.broadcasted_iota(jnp.int32, (1, slots), 1)
    for x in range(count_x):
        for y in range(count_y):
            for z in range(layers):
                at = slice(z, z + 1)
                for f in range(3):
                    own_ref[x, y, z, f : f + 1, :] = offsets_ref[f, x, y, at, :]
                    own_ref[x, y, z, 3 + f : 4 + f, :] = velocity_ref[f, x, y, at, :]
                own_ref[x, y, z, 6:7, :] = jnp.where(
                    lane < counts_ref[x, y, z], mass_ref[x, y, at, :], 0.0
                )
                own_ref[x, y, z, 7:8, :] = energy_ref[x, y, at, :]
    local = pltpu.make_async_copy(own_ref, ext_ref.at[interior], local_sem)
    local.start()
    pl.semaphore_wait(barrier, len(peers))
    copies = start_copies(peers, own_ref, ext_ref, count_x, count_y, send_sem, recv_sem)

    def enter(source, x, y, z, at):
        cell = source[at]
        rows = lax.broadcasted_iota(jnp.int32, cell.shape, 0)
        shift = jnp.where(rows == 0, float(x), jnp.where(rows == 1, float(y), float(z)))
        placed = jnp.where(rows < 3, (cell + shift) * (1.0 / SMOOTHING), cell)
        first = ((x * size_y + y) * layers + z) * slots
        list_ref[first : first + slots, 0:8] = placed.T
        return placed

    def gather(column, runs):
        mine = [
            jnp.concatenate([pack_ref[column, z, f : f + 1, :] for z in range(layers)], axis=1)
            for f in range(3)
        ]

        def body(step, total):
            cell, done = None, 0
            for first, cells in runs:
                here = first // layers + step - done
                cell = here if cell is None else jnp.where(step < done, cell, here)
                done += cells // layers
            rows = layers * slots
            near = list_ref[pl.ds(pl.multiple_of(cell * rows, rows), rows), 0:8]
            dist = None
            for f in range(3):
                gap = mine[f] - near[:, f : f + 1]
                dist = gap * gap if dist is None else dist + gap * gap
            q = dist * lax.rsqrt(jnp.maximum(dist, TINY))
            outer = jnp.maximum(2.0 - q, 0.0)
            inner = jnp.maximum(1.0 - q, 0.0)
            kernel = outer * outer * outer - 4.0 * (inner * inner * inner)
            return total + fold(kernel * near[:, 6:7])

        number = sum(cells // layers for _, cells in runs)
        return lax.fori_loop(0, number, body, jnp.zeros((8, layers * slots), jnp.float32))

    for column, (x, y) in enumerate(own):
        for z in range(layers):
            pack_ref[column, z, 0:8, :] = enter(own_ref, x, y, z, (x - 1, y - 1, z))
    for column, (x, y) in enumerate(own):
        runs = segments(x, y, inner_x, inner_y, layers, size_y, True)
        total_ref[column] = gather(column, runs)
    for copy in copies:
        copy.wait()
    for x in range(count_x + 2):
        for y in range(count_y + 2):
            if (x, y) not in own:
                for z in range(layers):
                    enter(ext_ref, x, y, z, (x, y, z))
    for column, (x, y) in enumerate(own):
        runs = segments(x, y, inner_x, inner_y, layers, size_y, False)
        total = total_ref[column] + gather(column, runs)
        value = jnp.sum(total, axis=0, keepdims=True) * (0.25 * NORMALISE)
        for z in range(layers):
            held = own_ref[x - 1, y - 1, z, 6:7, :] > 0.0
            row = value[:, z * slots : (z + 1) * slots]
            safe_ref[x - 1, y - 1, z : z + 1, :] = jnp.where(held, row, 1.0)
    local.wait()
    keep = pltpu.make_async_copy(safe_ref, near_ref.at[interior], local_sem)
    keep.start()
    copies = start_copies(peers, safe_ref, near_ref, count_x, count_y, rho_send, rho_recv)
    for x, y in own:
        for z in range(layers):
            index = (x - 1) * count_y + y - 1
            energy = own_ref[x - 1, y - 1, z, 7:8, :]
            pack_ref[index, z, 7:16, :] = thermal_rows(energy, safe_ref[x - 1, y - 1, z : z + 1, :])
            first = ((x * size_y + y) * layers + z) * slots
            list_ref[first : first + slots, 0:16] = pack_ref[index, z].T
    for column, (x, y) in enumerate(own):
        near_y = [b for b in (y - 1, y, y + 1) if b in inner_y]
        base = (x * size_y + near_y[0]) * layers
        mine = [
            jnp.concatenate([pack_ref[column, z, f : f + 1, :] for z in range(layers)], axis=1)
            for f in range(10)
        ]

        def body(step, sums, base=base, mine=mine):
            row = pl.multiple_of((base + step) * slots, slots)
            near = list_ref[pl.ds(row, slots), 0:16]
            return force_sums(mine, near, near[:, 6:7], sums)

        zeros = tuple(jnp.zeros((8, layers * slots), jnp.float32) for _ in range(4))
        sums = lax.fori_loop(0, len(near_y) * layers, body, zeros)
        for k in range(4):
            part_ref[column, k : k + 1, :] = jnp.sum(sums[k], axis=0, keepdims=True)
        part_ref[column, 4:8, :] = jnp.zeros((4, layers * slots), jnp.float32)
    keep.wait()
    for copy in copies:
        copy.wait()


def thermal_rows(energy, rho):
    return jnp.concatenate(
        [
            (ADIABATIC - 1.0) * energy / rho,
            jnp.sqrt(ADIABATIC * (ADIABATIC - 1.0) * energy) * (0.5 * VISC_ALPHA / VISC_BETA),
            rho * (1.0 / VISC_BETA),
            jnp.zeros((6, energy.shape[1]), jnp.float32),
        ],
        axis=0,
    )


def force_sums(mine, near, mass, sums):
    gaps, dist, approach = [], None, None
    for f in range(3):
        gap = mine[f] - near[:, f : f + 1]
        speed = mine[3 + f] - near[:, 3 + f : 4 + f]
        dist = gap * gap if dist is None else dist + gap * gap
        approach = gap * speed if approach is None else approach + gap * speed
        gaps.append(gap)
    inverse = lax.rsqrt(jnp.maximum(dist, TINY))
    q = dist * inverse
    outer = jnp.maximum(2.0 - q, 0.0)
    slope = jnp.where(q < 1.0, 4.0 - 3.0 * q, outer * outer * inverse)
    closing = jnp.minimum(approach, 0.0)
    soft = dist + SOFTENING
    sound = mine[8] + near[:, 8:9]
    dense = mine[9] + near[:, 9:10]
    half = closing * (closing - sound * soft) / (soft * soft * dense)
    from_own = mine[7] + half
    both = from_own + (near[:, 7:8] + half)
    weight = mass * slope
    push = weight * both
    heat = weight * from_own * approach
    return (
        sums[0] + fold(push * gaps[0]),
        sums[1] + fold(push * gaps[1]),
        sums[2] + fold(push * gaps[2]),
        sums[3] + fold(heat),
    )


def cell_counts(ext_ref, gap):
    size_x, size_y, layers = ext_ref.shape[:3]
    counts, starts, start = {}, {}, jnp.int32(0)
    for x in range(size_x):
        for y in range(size_y):
            for z in range(layers):
                held = jnp.where(ext_ref[x, y, z, 6:7, :] > 0.0, 1.0, 0.0)
                count = jnp.sum(held).astype(jnp.int32)
                counts[x, y, z] = count
                starts[x, y, z] = start
                start = start + (count + 7) // 8 * 8
            starts[x, y, layers] = start
        start = start + gap
    return counts, starts


def base_rows(ext_ref, x, y, z):
    cell = ext_ref[x, y, z]
    rows = lax.broadcasted_iota(jnp.int32, cell.shape, 0)
    shift = jnp.where(rows == 0, float(x), jnp.where(rows == 1, float(y), float(z)))
    placed = (cell + shift) * (1.0 / SMOOTHING)
    return jnp.where(rows < 3, placed, cell)


def fill_lists(features, keys, counts, starts, list_ref, pack_ref, chunk, layers, own):
    for key in keys:
        rows = features(key)
        first = pl.multiple_of(starts[key], 8)
        slots = rows.shape[1]
        list_ref[pl.ds(first, slots), 0 : rows.shape[0]] = rows.T
        if key[1:] == keys[-1][1:]:
            after = pl.multiple_of(first + slots, 8)
            list_ref[pl.ds(after, chunk), :] = jnp.zeros((chunk, list_ref.shape[1]), jnp.float32)
    for column, (x, y) in enumerate(own):
        lower, upper = features((x, y, 0)), features((x, y, 1))
        rolled = pltpu.roll(upper, jnp.bitwise_and(counts[x, y, 0], 127), 1)
        lane = lax.broadcasted_iota(jnp.int32, lower.shape, 1)
        pack_ref[column, 0] = jnp.where(lane < counts[x, y, 0], lower, rolled)
        pack_ref[column, 1] = rolled


def sweep(pair_body, n_sums, block_list, starts, x, y, inner_y, layers, chunk):
    spans = []
    for near_x in (x - 1, x, x + 1):
        skip = inner_y if near_x == x else ()
        for near_y in (y - 1, y, y + 1):
            if near_y in skip:
                continue
            first, end = starts[near_x, near_y, 0], starts[near_x, near_y, layers]
            if spans and spans[-1][0] == (near_x, near_y - 1):
                spans[-1] = ((near_x, near_y), spans[-1][1], end)
            else:
                spans.append(((near_x, near_y), first, end))
    total, below = jnp.int32(0), []
    for _, first, end in spans:
        below.append(total)
        total = total + (end - first + (chunk - 1)) // chunk

    def body(step, sums):
        row, last = spans[0][1] + step * chunk, spans[0][2]
        for before, (_, first, end) in zip(below[1:], spans[1:]):
            row = jnp.where(step < before, row, first + (step - before) * chunk)
            last = jnp.where(step < before, last, end)
        return pair_body(pl.multiple_of(row, 8), last, sums)

    width = 128 * block_list
    zeros = tuple(jnp.zeros((8, width), jnp.float32) for _ in range(n_sums))
    sums = lax.fori_loop(0, total, body, zeros)
    return [jnp.sum(s, axis=0, keepdims=True) for s in sums]


def fold(values):
    return jnp.sum(values.reshape(values.shape[0] // 8, 8, values.shape[1]), axis=0)


def unpack(row_a, row_b, count):
    back = jnp.bitwise_and(128 - jnp.bitwise_and(count, 127), 127)
    a = pltpu.roll(jnp.broadcast_to(row_a, (8, 128)), back, 1)[0:1]
    b = pltpu.roll(jnp.broadcast_to(row_b, (8, 128)), back, 1)[0:1]
    lane = lax.broadcasted_iota(jnp.int32, (1, 128), 1)
    upper = jnp.where(lane < 128 - count, a, b)
    return row_a, upper


def run_column(make_body, n_sums, total, out_ref, starts, x, y, inner_y, layers, chunks):
    @pl.when(total > 128)
    def _():
        sums = sweep(make_body(2, chunks[1]), n_sums, 2, starts, x, y, inner_y, layers, chunks[1])
        for k, row in enumerate(sums):
            out_ref[k : k + 1, :] = row

    @pl.when(total <= 128)
    def _():
        sums = sweep(make_body(1, chunks[0]), n_sums, 1, starts, x, y, inner_y, layers, chunks[0])
        for k, row in enumerate(sums):
            out_ref[k : k + 1, 0:128] = row
            out_ref[k : k + 1, 128:256] = jnp.zeros_like(row)


def own_columns(ext_ref):
    return [
        (x, y) for x in range(1, ext_ref.shape[0] - 1) for y in range(1, ext_ref.shape[1] - 1)
    ]


def all_cells(ext_ref):
    size_x, size_y, layers = ext_ref.shape[:3]
    return [(x, y, z) for x in range(size_x) for y in range(size_y) for z in range(layers)]


def wide(pack_ref, column, blocks, row):
    parts = [pack_ref[column, b, row : row + 1, :] for b in range(blocks)]
    return parts[0] if blocks == 1 else jnp.concatenate(parts, axis=1)


def force_kernel(
    chunks, ext_ref, rho_ref, part_ref, density_ref, accel_ref, heat_ref, feat_ref, list_ref, pack_ref, sum_ref
):
    layers = ext_ref.shape[2]
    counts, starts = cell_counts(ext_ref, max(chunks))
    own = own_columns(ext_ref)
    inner_y = range(1, ext_ref.shape[1] - 1)

    for key in all_cells(ext_ref):
        x, y, z = key
        energy = ext_ref[x, y, z, 7:8, :]
        rho = rho_ref[x, y, z : z + 1, :]
        feat_ref[x, y, z, 0:8, :] = base_rows(ext_ref, x, y, z)
        feat_ref[x, y, z, 7:16, :] = thermal_rows(energy, rho)
    fill_lists(
        lambda key: feat_ref[key],
        all_cells(ext_ref), counts, starts, list_ref, pack_ref, max(chunks), layers, own,
    )
    for column, (x, y) in enumerate(own):

        def make_body(blocks, chunk, column=column):
            mine = [wide(pack_ref, column, blocks, f) for f in range(10)]

            def body(row, end, sums):
                near = list_ref[pl.ds(row, chunk), 0:16]
                place = lax.broadcasted_iota(jnp.int32, near.shape, 0)
                mass = jnp.where(place < end - row, near, 0.0)[:, 6:7]
                return force_sums(mine, near, mass, sums)

            return body

        count = counts[x, y, 0]
        run_column(
            make_body, 4, count + counts[x, y, 1], sum_ref, starts, x, y, inner_y, layers, chunks
        )
        for z in range(layers):
            held = ext_ref[x, y, z, 6:7, :] > 0.0
            density_ref[x - 1, y - 1, z : z + 1, :] = jnp.where(held, rho_ref[x, y, z : z + 1, :], 0.0)
        factor = 0.75 * NORMALISE / SMOOTHING
        for k in range(4):
            rows = unpack(sum_ref[k : k + 1, 0:128], sum_ref[k : k + 1, 128:256], count)
            for z in range(layers):
                held = ext_ref[x, y, z, 6:7, :] > 0.0
                value = rows[z] + part_ref[column, k : k + 1, z * 128 : (z + 1) * 128]
                if k < 3:
                    accel_ref[k, x - 1, y - 1, z : z + 1, :] = jnp.where(held, value * factor, 0.0)
                else:
                    heat_ref[x - 1, y - 1, z : z + 1, :] = jnp.where(held, value * -factor, 0.0)


def shards(offsets, velocity, mass, energy, counts):
    slots = mass.shape[-1]
    count_x, count_y, layers = mass.shape[:3]
    wide_x, wide_y = count_x + 2, count_y + 2
    cells = wide_x * wide_y * layers
    own = count_x * count_y
    vmem = pl.BlockSpec(memory_space=VMEM)
    sems = pltpu.SemaphoreType.DMA((len(DIRECTIONS),))
    own_shape = (count_x, count_y, layers, 8, slots)
    extended, near, part = pl.pallas_call(
        functools.partial(density_kernel, lax.axis_size("gx"), lax.axis_size("gy")),
        out_shape=[
            jax.ShapeDtypeStruct((wide_x, wide_y) + own_shape[2:], jnp.float32),
            jax.ShapeDtypeStruct((wide_x, wide_y, layers, slots), jnp.float32),
            jax.ShapeDtypeStruct((own, 8, layers * slots), jnp.float32),
        ],
        in_specs=[pl.BlockSpec(memory_space=pl.ANY)] * 4 + [pl.BlockSpec(memory_space=pltpu.SMEM)],
        out_specs=[vmem, vmem, vmem],
        scratch_shapes=[
            VMEM(offsets.shape, jnp.float32),
            VMEM(velocity.shape, jnp.float32),
            VMEM(mass.shape, jnp.float32),
            VMEM(energy.shape, jnp.float32),
            VMEM(own_shape, jnp.float32),
            VMEM((cells * slots, 128), jnp.float32),
            VMEM((own, layers, 16, slots), jnp.float32),
            VMEM((own, 8, layers * slots), jnp.float32),
            VMEM((count_x, count_y, layers, slots), jnp.float32),
            sems,
            sems,
            sems,
            sems,
            pltpu.SemaphoreType.DMA,
            pltpu.SemaphoreType.DMA((4,)),
        ],
        compiler_params=pltpu.CompilerParams(collective_id=0, has_side_effects=True),
        name="density",
    )(offsets, velocity, mass, energy, counts)
    force_chunks = (128, 64)
    density, accel, heat = pl.pallas_call(
        functools.partial(force_kernel, force_chunks),
        out_shape=[
            jax.ShapeDtypeStruct(mass.shape, jnp.float32),
            jax.ShapeDtypeStruct((3,) + mass.shape, jnp.float32),
            jax.ShapeDtypeStruct(mass.shape, jnp.float32),
        ],
        in_specs=[vmem, vmem, vmem],
        out_specs=[vmem, vmem, vmem],
        scratch_shapes=[
            VMEM((wide_x, wide_y, layers, 16, slots), jnp.float32),
            VMEM((cells * slots + wide_x * max(force_chunks), 128), jnp.float32),
            VMEM((own, 2, 16, slots), jnp.float32),
            VMEM((8, 2 * slots), jnp.float32),
        ],
        name="force",
    )(extended, near, part)
    return (density, accel, heat)


def solution(mesh):
    in_specs = (
        P(None, "gx", "gy", None, None),
        P(None, "gx", "gy", None, None),
        P("gx", "gy", None, None),
        P("gx", "gy", None, None),
        P("gx", "gy", None),
    )
    out_specs = (
        P("gx", "gy", None, None),
        P(None, "gx", "gy", None, None),
        P("gx", "gy", None, None),
    )
    return jax.shard_map(shards, mesh=mesh, in_specs=in_specs, out_specs=out_specs, check_vma=False)
```
